256 devices in a mesh: seq: 32 (over x, z), head: 8 (over y, core).
Axes of the slice: x: 4, y: 4, z: 8, core: 2. Of those that a mesh axis runs over, the one named last changes fastest.
Arguments:
- queries: bfloat16 [65536, 4096], P(('seq', 'head')), may hold values from -6 to 6
- keys: bfloat16 [65536, 4096], P(('seq', 'head')), may hold values from -6 to 6
- values: bfloat16 [65536, 4096], P(('seq', 'head')), may hold values from -6 to 6
- spikes: int32 [65536, 4096], P(('seq', 'head')), may hold values from 0 to 26
- gain: float32 [4096], P('head'), may hold values from 0.1 to 1.9
Outputs:
- attended: bfloat16 [65536, 4096], P('seq', 'head')
- cache: float32 [32, 32, 128, 128], P('seq', 'head')
The draws below stay inside these ranges and needn't reach their ends.
Inputs may be any that keep to these rules, and one draw needn't show every extreme that they name: spikes codes count_query + 3 count_key + 9 count_value with each count 0, 1 or 2.
All inputs are finite; a program needn't handle non-finite values.
Results may differ from the reference program's by a relative error of at most 0.0027.
Values may be sent and summed in bfloat16 or wider, within the bound.
A program may use at most 128 MiB of HBM per device.

```python
import jax
import jax.numpy as jnp
from jax import lax

HEADS = 32
HD = 128
D = 4096
BLOCK = 2048
BLOCKS = 32
TOKENS = 65536


def set_ends(entries, rng, smallest, high):
    spot = [jax.random.randint(jax.random.fold_in(rng, axis), (), 0, length) for axis, length in enumerate(entries.shape)]
    main_axis = entries.shape.index(max(entries.shape))
    neighbour = spot[:main_axis] + [(spot[main_axis] + 1) % entries.shape[main_axis]] + spot[main_axis + 1:]
    return entries.at[tuple(spot)].set(smallest).at[tuple(neighbour)].set(high)


def level_of(rng, shape, shards, low, largest):
    level = 1.0
    for position, shards_of in shards:
        draws = jax.random.uniform(jax.random.fold_in(jax.random.fold_in(rng, 6), position), (shards_of,), jnp.float32, low / len(shards), largest / len(shards))
        level = level * jnp.repeat(jnp.exp(draws), shape[position] // shards_of).reshape((-1,) + (1,) * (len(shape) - 1 - position))
    return level


def gaussian(stream_key, dims, width, reach, cuts=(), kind=jnp.bfloat16):
    factor_of = level_of(stream_key, dims, cuts, -0.22, 0.18) if cuts else 1.0
    array = jax.random.normal(stream_key, dims, jnp.float32) * width * factor_of
    return jnp.minimum(jnp.maximum(array, -reach), reach).astype(kind)


def setup_inputs(seed: int = 0) -> dict:
    seeds = jax.random.split(jax.random.key(seed), 6)
    return {
        "queries": gaussian(seeds[0], (TOKENS, D), 1.0, 6.0, ((0, 256),)),
        "keys": gaussian(seeds[1], (TOKENS, D), 1.0, 6.0, ((0, 256),)),
        "values": gaussian(seeds[2], (TOKENS, D), 1.0, 6.0, ((0, 256),)),
        "spikes": set_ends(jax.random.randint(seeds[3], (TOKENS, D), 0, 27), jax.random.fold_in(seeds[3], 1), 0, 26).astype(jnp.int32),
        "gain": jnp.clip(1.0 + 0.18 * jax.random.normal(seeds[4], (D,), jnp.float32), 0.1, 1.9),
    }


def decode_counts(spikes):
    return (spikes % 3, spikes // 3 % 3, spikes // 9)

def reference(queries, keys, values, spikes, gain):
    count_query, count_key, count_value = decode_counts(spikes)
    spiked_query = queries * count_query.astype(queries.dtype)
    spiked_key = keys * count_key.astype(keys.dtype)
    spiked_value = values * count_value.astype(values.dtype)
    score_scale = HD ** (-0.5)
    causal = lax.broadcasted_iota(jnp.int32, (BLOCK, BLOCK), 0) >= lax.broadcasted_iota(jnp.int32, (BLOCK, BLOCK), 1)

    def one_head(head):
        start = (head * HD).astype(jnp.int32)
        query_blocks = lax.dynamic_slice_in_dim(spiked_query, start, HD, 1).reshape(BLOCKS, BLOCK, HD)
        key_blocks = lax.dynamic_slice_in_dim(spiked_key, start, HD, 1).reshape(BLOCKS, BLOCK, HD)
        value_blocks = lax.dynamic_slice_in_dim(spiked_value, start, HD, 1).reshape(BLOCKS, BLOCK, HD)
        states = jnp.einsum('nsd,nse->nde', key_blocks.astype(jnp.float32), value_blocks.astype(jnp.float32), precision=lax.Precision.HIGHEST)
        inclusive = jnp.cumsum(states, axis=0)
        earlier = jnp.concatenate([jnp.zeros((1, HD, HD), jnp.float32), inclusive[:-1]], axis=0)

        def one_block(pieces):
            query_rows, key_rows, value_rows, carried_state = pieces
            scores = jnp.dot(query_rows, key_rows.T, preferred_element_type=jnp.float32) * score_scale
            weights = jnp.where(causal, scores, 0.0).astype(jnp.bfloat16)
            local_part = jnp.dot(weights, value_rows, preferred_element_type=jnp.float32)
            carried = jnp.dot(query_rows.astype(jnp.float32), carried_state, precision=lax.Precision.HIGHEST) * score_scale
            return local_part + carried
        raw = lax.map(one_block, (query_blocks, key_blocks, value_blocks, earlier)).reshape(TOKENS, HD)
        head_gain = lax.dynamic_slice_in_dim(gain, start, HD, 0)
        normed = raw * lax.rsqrt(lax.optimization_barrier(jnp.mean(raw * raw, axis=-1, keepdims=True)) + 1e-06) * head_gain
        seen_tokens = ((jnp.arange(BLOCKS, dtype=jnp.int32) + 1) * BLOCK).astype(jnp.float32)
        scaled = inclusive * lax.rsqrt(seen_tokens)[:, None, None]
        return (normed.astype(jnp.bfloat16), scaled)
    outputs, caches = lax.map(one_head, jnp.arange(HEADS, dtype=jnp.int32))
    attended = outputs.transpose(1, 0, 2).reshape(TOKENS, HEADS * HD)
    return (attended, caches.transpose(1, 0, 2, 3))
```

```python
import functools

import jax
import jax.numpy as jnp
from jax import lax
from jax.experimental import pallas as pl
from jax.experimental.pallas import tpu as pltpu
from jax.sharding import PartitionSpec as P

HD = 128
NX, NZ, NY, NC = 4, 8, 4, 2
NH = NY * NC
NK = 4
ROWS = 256
BLOCK = 2048
ZR = HD // NZ
SCALE = HD ** (-0.5)
f32, bf16 = jnp.float32, jnp.bfloat16


def dot(a, b, dims):
    return lax.dot_general(a, b, (dims, ((), ())), preferred_element_type=f32)


def kernel(q_ref, k_ref, v_ref, sp_ref, g_ref, out_ref, cache_ref,
           qb, kb, vb, sb, lb, S, RC, CS, T1, TZ, Z1, ZT, XB, E2, EB, PB, T3, PF, SP, OB, GB,
           in_sem, own_sem, g_s, g_r, c1_s, c1_r, t1_s, t1_r, z1_s, z1_r, x_s, x_r, z2_s, z2_r,
           t3_s, t3_r, c2_s, c2_r, o_s, o_r):
    s = lax.axis_index("seq")
    h = lax.axis_index("head")
    x, z = s // NZ, s % NZ
    y, c = h // NC, h % NC

    def at_y(d):
        return s, ((y + d) % NY) * NC + c

    def at_h(d):
        return s, (h + d) % NH

    def at_z(d):
        return x * NZ + (z + d) % NZ, h

    def at_x(d):
        return ((x + d) % NX) * NZ + z, h

    partner = (s, y * NC + 1 - c)

    def dev(p):
        return {"seq": p[0], "head": p[1]}

    sent = []

    def send(src, dst, ss, rs, to):
        cp = pltpu.make_async_remote_copy(src_ref=src, dst_ref=dst, send_sem=ss, recv_sem=rs,
                                          device_id=dev(to), device_id_type=pl.DeviceIdType.MESH)
        cp.start()
        sent.append(cp)
        return cp

    peers = [at_h(d) for d in range(1, NH)] + [at_z(d) for d in range(1, NZ)] + [at_x(d) for d in range(1, NX)]
    barrier = pltpu.get_barrier_semaphore()
    for p in peers:
        pl.semaphore_signal(barrier, inc=1, device_id=dev(p), device_id_type=pl.DeviceIdType.MESH)

    arrays = ((sp_ref, sb), (q_ref, qb), (k_ref, kb), (v_ref, vb))
    for k in range(NK):
        for a, (src, dst) in enumerate(arrays):
            for g in range(NH):
                pltpu.make_async_copy(src.at[:, pl.ds((g * NK + k) * HD, HD)], dst.at[k, g], in_sem.at[k, a]).start()

    c1, t1, z1, xc, z2, t3, c2, oc = ({} for _ in range(8))

    def stage_a(k):
        for a, (src, dst) in enumerate(arrays):
            pltpu.make_async_copy(dst.at[k], dst.at[k], in_sem.at[k, a]).wait()

        def decode(i, _):
            g = i // 4
            rows = pl.ds(pl.multiple_of((i % 4) * 64, 64), 64)
            t = sb[k, g, rows, :].astype(f32)
            cv = jnp.floor(t * 0.1112)
            r = t - 9.0 * cv
            ck = jnp.floor(r * 0.334)
            cq = r - 3.0 * ck
            qb[k, g, rows, :] = qb[k, g, rows, :] * cq.astype(bf16)
            kb[k, g, rows, :] = kb[k, g, rows, :] * ck.astype(bf16)
            vb[k, g, rows, :] = vb[k, g, rows, :] * cv.astype(bf16)
            return 0

        lax.fori_loop(0, NH * 4, decode, 0, unroll=2)

        def states(yy, _):
            for cc in range(NC):
                S[k, cc, yy] = dot(kb[k, yy * NC + cc], vb[k, yy * NC + cc], ((0,), (0,)))
            return 0

        lax.fori_loop(0, NY, states, 0)

    def send_a(k):
        c1[k] = send(S.at[k, 1 - c], RC.at[k], c1_s.at[k], c1_r.at[k], partner)

    def stage_c(k):
        c1[k].wait_recv()
        for yy in range(NY):
            CS[k, yy] = S[k, c, yy] + RC[k, yy]
        t1[k] = [send(CS.at[k, (y + d) % NY], T1.at[k, y], t1_s.at[k, d - 1], t1_r.at[k, d - 1], at_y(d)) for d in range(1, NY)]
        T1[k, y] = CS[k, y]

    def stage_l(k):
        causal = lax.broadcasted_iota(jnp.int32, (ROWS, ROWS), 0) >= lax.broadcasted_iota(jnp.int32, (ROWS, ROWS), 1)

        def local(g, _):
            scores = dot(qb[k, g], kb[k, g], ((1,), (1,))) * SCALE
            weights = jnp.where(causal, scores, 0.0).astype(bf16)
            lb[k, g] = dot(weights, vb[k, g], ((1,), (0,)))
            return 0

        lax.fori_loop(0, NH, local, 0)

    def stage_d(k):
        for cp in t1[k]:
            cp.wait_recv()
        total = T1[k, 0] + T1[k, 1] + T1[k, 2] + T1[k, 3]
        TZ[k] = total.reshape(NZ, ZR, HD)
        z1[k] = [send(TZ.at[k, (z + d) % NZ], Z1.at[k, z], z1_s.at[k, d - 1], z1_r.at[k, d - 1], at_z(d)) for d in range(1, NZ)]
        Z1[k, z] = TZ[k, z]

    def stage_x(k):
        for cp in z1[k]:
            cp.wait_recv()
        total = Z1[k, 0]
        for zz in range(1, NZ):
            total = total + Z1[k, zz]
        ZT[k] = total
        xc[k] = [send(ZT.at[k], XB.at[k, x], x_s.at[k, d - 1], x_r.at[k, d - 1], at_x(d)) for d in range(1, NX)]
        XB[k, x] = total

    def stage_y(k):
        for cp in xc[k]:
            cp.wait_recv()
        run = jnp.zeros((ZR, HD), f32)
        for xx in range(NX - 1):
            run = run + jnp.where(xx < x, XB[k, xx], 0.0)
        for zz in range(NZ):
            E2[k, zz] = run
            run = run + Z1[k, zz]
        z2[k] = [send(E2.at[k, (z + d) % NZ], EB.at[k, z], z2_s.at[k, d - 1], z2_r.at[k, d - 1], at_z(d)) for d in range(1, NZ)]
        EB[k, z] = E2[k, z]

    def stage_f(k):
        for cp in z2[k]:
            cp.wait_recv()
        run = EB[k].reshape(HD, HD)
        for yy in range(NY):
            PB[k, yy] = run
            run = run + T1[k, yy]
        t3[k] = [send(PB.at[k, (y + d) % NY], T3.at[k, y], t3_s.at[k, d - 1], t3_r.at[k, d - 1], at_y(d)) for d in range(1, NY)]
        T3[k, y] = PB[k, y]
        seen = jnp.full((8, HD), (s + 1) * BLOCK, jnp.int32).astype(f32)
        cache_ref[0, k] = (run.reshape(HD // 8, 8, HD) * lax.rsqrt(seen)).reshape(HD, HD)

    def stage_g(k):
        for cp in t3[k]:
            cp.wait_recv()
        for yy in range(NY):
            base = T3[k, yy]
            first = jnp.where(c == 0, S[k, 0, yy], RC[k, yy])
            after = base + first
            PF[k, c, yy] = jnp.where(c == 0, base, after)
            SP[k, yy] = jnp.where(c == 0, after, base)
        c2[k] = send(SP.at[k], PF.at[k, c], c2_s.at[k], c2_r.at[k], partner)

    def stage_h(k):
        c2[k].wait_recv()

        def final(yy, _):
            for cc in range(NC):
                g = yy * NC + cc
                p = PF[k, cc, yy]
                hi = p.astype(bf16)
                lo = (p - hi.astype(f32)).astype(bf16)
                q = qb[k, g]
                carried = dot(jnp.concatenate([q, q], axis=1), jnp.concatenate([hi, lo], axis=0), ((1,), (0,)))
                raw = lb[k, g] + carried * SCALE
                mean = jnp.mean(raw * raw, axis=-1, keepdims=True)
                normed = raw * lax.rsqrt(mean + 1e-06) * GB[g, pl.ds(k, 1), :]
                OB[k, g] = normed.astype(bf16)
            return 0

        lax.fori_loop(0, NY, final, 0)
        here = out_ref.at[pl.ds(h * ROWS, ROWS), pl.ds(k * HD, HD)]
        oc[k] = [send(OB.at[k, (h + d) % NH], here, o_s.at[k, d - 1], o_r.at[k, d - 1], at_h(d)) for d in range(1, NH)]
        own = pltpu.make_async_copy(OB.at[k, h], here, own_sem.at[k])
        own.start()
        return own

    stage_a(0)
    pl.semaphore_wait(barrier, len(peers))
    send_a(0)
    GB[h] = g_ref[...]
    gains = [send(g_ref, GB.at[h], g_s.at[d - 1], g_r.at[d - 1], at_h(d)) for d in range(1, NH)]
    stage_a(1)
    send_a(1)
    stage_c(0)
    stage_a(2)
    send_a(2)
    stage_c(1)
    stage_a(3)
    send_a(3)
    stage_c(2)
    stage_c(3)
    stage_l(0)
    stage_d(0)
    stage_l(1)
    stage_d(1)
    stage_x(0)
    stage_l(2)
    stage_d(2)
    stage_x(1)
    stage_y(0)
    stage_l(3)
    stage_d(3)
    stage_x(2)
    stage_y(1)
    stage_f(0)
    stage_x(3)
    stage_y(2)
    stage_f(1)
    stage_y(3)
    stage_g(0)
    stage_f(2)
    for cp in gains:
        cp.wait_recv()
    own = [stage_h(0)]
    stage_g(1)
    stage_f(3)
    own.append(stage_h(1))
    stage_g(2)
    own.append(stage_h(2))
    stage_g(3)
    own.append(stage_h(3))
    for k in range(NK):
        own[k].wait()
        for cp in oc[k]:
            cp.wait_recv()
    for cp in sent:
        cp.wait_send()


def per_device(queries, keys, values, spikes, gain):
    vmem, dma = pltpu.VMEM, pltpu.SemaphoreType.DMA
    anywhere = pl.BlockSpec(memory_space=pl.ANY)
    inside = pl.BlockSpec(memory_space=pltpu.VMEM)
    state = vmem((NK, NY, HD, HD), f32)
    slices = vmem((NK, NZ, ZR, HD), f32)
    counts = (NH - 1,), (NK,), (NK, NY - 1), (NK, NZ - 1), (NK, NX - 1), (NK, NZ - 1), (NK, NY - 1), (NK,), (NK, NH - 1)
    attended, cache = pl.pallas_call(
        kernel,
        out_shape=(jax.ShapeDtypeStruct((BLOCK, NK * HD), bf16), jax.ShapeDtypeStruct((1, NK, HD, HD), f32)),
        in_specs=[anywhere] * 4 + [inside],
        out_specs=(anywhere, inside),
        scratch_shapes=[
            vmem((NK, NH, ROWS, HD), bf16), vmem((NK, NH, ROWS, HD), bf16), vmem((NK, NH, ROWS, HD), bf16),
            vmem((NK, NH, ROWS, HD), jnp.int32), vmem((NK, NH, ROWS, HD), f32),
            vmem((NK, NC, NY, HD, HD), f32), state, state, state,
            slices, slices, vmem((NK, ZR, HD), f32), vmem((NK, NX, ZR, HD), f32), slices, slices,
            state, state, vmem((NK, NC, NY, HD, HD), f32), state,
            vmem((NK, NH, ROWS, HD), bf16), vmem((NH, NK, HD), f32),
            dma((NK, 4)), dma((NK,)),
        ] + [dma(n) for n in counts for _ in range(2)],
        compiler_params=pltpu.CompilerParams(collective_id=0, has_side_effects=True, vmem_limit_bytes=60 << 20),
    )(queries, keys, values, spikes, gain.reshape(NK, HD))
    return attended, cache


def solution(mesh):
    tokens = P(("seq", "head"), None)
    return jax.shard_map(
        per_device, mesh=mesh, in_specs=(tokens, tokens, tokens, tokens, P("head")),
        out_specs=(P("seq", "head"), P("seq", "head", None, None)), check_vma=False,
    )
```

```python
import functools

import jax
import jax.numpy as jnp
from jax import lax
from jax.experimental import pallas as pl
from jax.experimental.pallas import tpu as pltpu
from jax.sharding import PartitionSpec as P

HD = 128
NX, NZ, NY, NC = 4, 8, 4, 2
NH = NY * NC
NK = 4
ROWS = 256
BLOCK = 2048
ZR = HD // NZ
SCALE = HD ** (-0.5)
LAST = NK - 1
ORDER = (
    "a0", "b0", "s0", "a1", "s1", "c0", "a2", "s2", "c1", "a3", "s3", "c2", "c3", "q3",
    "l3", "d0", "d1", "l0", "d2", "d3", "x0", "x1", "l1", "y0", "x2", "y1", "l2", "x3",
    "y2", "f0", "y3", "f1", "f2", "g0", "h0", "g1", "f3", "h1", "g2", "h2", "w3",
)
f32, bf16 = jnp.float32, jnp.bfloat16


def dot(a, b, dims):
    return lax.dot_general(a, b, (dims, ((), ())), preferred_element_type=f32)


def encode(state):
    top = jnp.max(jnp.abs(state), axis=0, keepdims=True)
    scaled = state * jnp.where(top > 0.0, 1.0 / jnp.where(top > 0.0, top, 1.0), 0.0) * 32767.0
    return jnp.floor(scaled + 0.5).astype(jnp.int32).astype(jnp.int16), top


def decode_state(code, top):
    return code.astype(jnp.int32).astype(f32) * (1.0 / 32767.0) * top


def kernel(q_ref, k_ref, v_ref, sp_ref, g_ref, out_ref, cache_ref,
           qb, kb, vb, sb, lb, S, RC, CC, CM, RT, RM, T1, TZ, Z1, ZT, XB, E2, EB, PB, PC, PM, T3, TM, PF, SP, OB, GB,
           QX, LO, LX, WO,
           in_sem, own_sem, g_s, g_r, c1_s, c1_r, t1_s, t1_r, z1_s, z1_r, x_s, x_r, z2_s, z2_r,
           t3_s, t3_r, c2_s, c2_r, o_s, o_r, q_s, q_r, l_s, l_r):
    s = lax.axis_index("seq")
    h = lax.axis_index("head")
    x, z = s // NZ, s % NZ
    y, c = h // NC, h % NC

    def at_y(d):
        return s, ((y + d) % NY) * NC + c

    def at_h(d):
        return s, (h + d) % NH

    def at_z(d):
        return x * NZ + (z + d) % NZ, h

    def at_x(d):
        return ((x + d) % NX) * NZ + z, h

    partner = (s, y * NC + 1 - c)

    def dev(p):
        return {"seq": p[0], "head": p[1]}

    sent, own, gains, arrived = [], [], [], set()

    def arrive(copies):
        for cp in copies:
            cp.wait_recv()
            arrived.add(id(cp))

    def send(src, dst, ss, rs, to):
        cp = pltpu.make_async_remote_copy(src_ref=src, dst_ref=dst, send_sem=ss, recv_sem=rs,
                                          device_id=dev(to), device_id_type=pl.DeviceIdType.MESH)
        cp.start()
        sent.append(cp)
        return cp

    peers = [at_h(d) for d in range(1, NH)] + [at_z(d) for d in range(1, NZ)] + [at_x(d) for d in range(1, NX)]
    barrier = pltpu.get_barrier_semaphore()
    for p in peers:
        pl.semaphore_signal(barrier, inc=1, device_id=dev(p), device_id_type=pl.DeviceIdType.MESH)

    arrays = ((sp_ref, sb), (q_ref, qb), (k_ref, kb), (v_ref, vb))
    for k in range(NK):
        for a, (src, dst) in enumerate(arrays):
            for g in range(NH):
                pltpu.make_async_copy(src.at[:, pl.ds((g * NK + k) * HD, HD)], dst.at[k, g], in_sem.at[k, a]).start()

    c1, t1, z1, xc, z2, t3, c2, oc, ql = ({} for _ in range(9))

    def stage_a(k):
        for a, (src, dst) in enumerate(arrays):
            pltpu.make_async_copy(dst.at[k], dst.at[k], in_sem.at[k, a]).wait()

        def decode(i, _):
            g = i // 4
            rows = pl.ds(pl.multiple_of((i % 4) * 64, 64), 64)
            t = sb[k, g, rows, :].astype(f32)
            cv = jnp.floor(t * 0.1112)
            r = t - 9.0 * cv
            ck = jnp.floor(r * 0.334)
            cq = r - 3.0 * ck
            qb[k, g, rows, :] = qb[k, g, rows, :] * cq.astype(bf16)
            kb[k, g, rows, :] = kb[k, g, rows, :] * ck.astype(bf16)
            vb[k, g, rows, :] = vb[k, g, rows, :] * cv.astype(bf16)
            return 0

        lax.fori_loop(0, NH * 4, decode, 0, unroll=2)

        def states(yy, _):
            for cc in range(NC):
                S[k, cc, yy] = dot(vb[k, yy * NC + cc], kb[k, yy * NC + cc], ((0,), (0,)))
            return 0

        lax.fori_loop(0, NY, states, 0)

    def send_a(k):
        if k == LAST:
            c1[k] = send(S.at[k], RC.at[pl.ds(2 * k, 2)], c1_s.at[k], c1_r.at[k], partner)
        else:
            c1[k] = send(S.at[k, 1 - c], RC.at[2 * k + 1 - c], c1_s.at[k], c1_r.at[k], partner)

    def stage_c(k):
        arrive([c1[k]])
        for yy in range(NY):
            CC[k, yy], CM[k, yy] = encode(S[k, c, yy] + RC[2 * k + c, yy])
        t1[k] = []
        for d in range(1, NY):
            to = (y + d) % NY
            t1[k].append(send(CC.at[k, to], RT.at[k, y], t1_s.at[k, d - 1, 0], t1_r.at[k, d - 1, 0], at_y(d)))
            t1[k].append(send(CM.at[k, to], RM.at[k, y], t1_s.at[k, d - 1, 1], t1_r.at[k, d - 1, 1], at_y(d)))
        RT[k, y] = CC[k, y]
        RM[k, y] = CM[k, y]

    def apply_state(q, state):
        hi = state.astype(bf16)
        lo = (state - hi.astype(f32)).astype(bf16)
        return dot(jnp.concatenate([q, q], axis=1), jnp.concatenate([hi, lo], axis=1), ((1,), (1,))) * SCALE

    def stage_l(k):
        causal = lax.broadcasted_iota(jnp.int32, (ROWS, ROWS), 0) >= lax.broadcasted_iota(jnp.int32, (ROWS, ROWS), 1)
        second = c.astype(f32)

        def local(yy, _):
            for cc in range(NC):
                g = yy * NC + cc
                scores = dot(qb[k, g], kb[k, g], ((1,), (1,))) * SCALE
                weights = jnp.where(causal, scores, 0.0).astype(bf16)
                part = dot(weights, vb[k, g], ((1,), (0,)))
                if k == LAST:
                    part = part + apply_state(qb[k, g], RC[2 * k + cc, yy] * second)
                    LO[g] = part.astype(bf16)
                else:
                    lb[k, g] = part
            return 0

        lax.fori_loop(0, NY, local, 0)
        if k == LAST:
            for d in range(1, NH):
                ql[k].append(send(LO.at[(h + d) % NH], LX.at[h], l_s.at[d - 1], l_r.at[d - 1], at_h(d)))
            LX[h] = LO[h]

    def stage_q(k):
        ql[k] = [send(qb.at[k, (h + d) % NH], QX.at[h], q_s.at[d - 1], q_r.at[d - 1], at_h(d)) for d in range(1, NH)]
        QX[h] = qb[k, h]

    def stage_d(k):
        arrive(t1[k])
        total = None
        for yy in range(NY):
            part = decode_state(RT[k, yy], RM[k, yy])
            T1[k, yy] = part
            total = part if total is None else total + part
        TZ[k] = total.reshape(NZ, ZR, HD)
        z1[k] = [send(TZ.at[k, (z + d) % NZ], Z1.at[k, z], z1_s.at[k, d - 1], z1_r.at[k, d - 1], at_z(d)) for d in range(1, NZ)]
        Z1[k, z] = TZ[k, z]

    def stage_x(k):
        arrive(z1[k])
        total = Z1[k, 0]
        for zz in range(1, NZ):
            total = total + Z1[k, zz]
        ZT[k] = total
        xc[k] = [send(ZT.at[k], XB.at[k, x], x_s.at[k, d - 1], x_r.at[k, d - 1], at_x(d)) for d in range(1, NX)]
        XB[k, x] = total

    def stage_y(k):
        arrive(xc[k])
        run = jnp.zeros((ZR, HD), f32)
        for xx in range(NX - 1):
            run = run + jnp.where(xx < x, XB[k, xx], 0.0)
        for zz in range(NZ):
            E2[k, zz] = run
            run = run + Z1[k, zz]
        z2[k] = [send(E2.at[k, (z + d) % NZ], EB.at[k, z], z2_s.at[k, d - 1], z2_r.at[k, d - 1], at_z(d)) for d in range(1, NZ)]
        EB[k, z] = E2[k, z]

    def stage_f(k):
        arrive(z2[k])
        run = EB[k].reshape(HD, HD)
        for yy in range(NY):
            if k == LAST:
                PB[yy] = run
            else:
                PC[k, yy], PM[k, yy] = encode(run)
            run = run + T1[k, yy]
        t3[k] = []
        if k != LAST:
            for d in range(1, NY):
                to = (y + d) % NY
                t3[k].append(send(PC.at[k, to], T3.at[k, y], t3_s.at[k, d - 1, 0], t3_r.at[k, d - 1, 0], at_y(d)))
                t3[k].append(send(PM.at[k, to], TM.at[k, y], t3_s.at[k, d - 1, 1], t3_r.at[k, d - 1, 1], at_y(d)))
            T3[k, y] = PC[k, y]
            TM[k, y] = PM[k, y]
        seen = jnp.full((8, HD), (s + 1) * BLOCK, jnp.int32).astype(f32)
        cache_ref[0, k] = (run.T.reshape(HD // 8, 8, HD) * lax.rsqrt(seen)).reshape(HD, HD)

    def stage_g(k):
        arrive(t3[k])
        for yy in range(NY):
            base = decode_state(T3[k, yy], TM[k, yy])
            after = base + jnp.where(c == 0, S[k, 0, yy], RC[2 * k + 1, yy])
            PF[k, c, yy] = jnp.where(c == 0, base, after)
            SP[k, yy] = jnp.where(c == 0, after, base)
        c2[k] = send(SP.at[k], PF.at[k, c], c2_s.at[k], c2_r.at[k], partner)

    def normed(raw, gain):
        mean = jnp.mean(raw * raw, axis=-1, keepdims=True)
        return (raw * lax.rsqrt(mean + 1e-06) * gain).astype(bf16)

    def stage_h(k):
        arrive([c2[k]] + gains if k == 0 else [c2[k]])

        def final(yy, _):
            for cc in range(NC):
                g = yy * NC + cc
                OB[k, g] = normed(lb[k, g] + apply_state(qb[k, g], PF[k, cc, yy]), GB[g, pl.ds(k, 1), :])
            return 0

        lax.fori_loop(0, NY, final, 0)
        here = out_ref.at[pl.ds(h * ROWS, ROWS), pl.ds(k * HD, HD)]
        oc[k] = [send(OB.at[k, (h + d) % NH], here, o_s.at[k, d - 1], o_r.at[k, d - 1], at_h(d)) for d in range(1, NH)]
        mine = pltpu.make_async_copy(OB.at[k, h], here, own_sem.at[k])
        mine.start()
        own.append(mine)

    def stage_w(k):
        arrive(ql[k])

        def final(yy, _):
            for cc in range(NC):
                g = yy * NC + cc
                WO[g] = normed(LX[g].astype(f32) + apply_state(QX[g], PB[yy]), g_ref[pl.ds(k, 1), :])
            return 0

        lax.fori_loop(0, NY, final, 0)
        for g in range(NH):
            mine = pltpu.make_async_copy(WO.at[g], out_ref.at[pl.ds(g * ROWS, ROWS), pl.ds(k * HD, HD)], own_sem.at[NK + g])
            mine.start()
            own.append(mine)

    def stage_b(_):
        pl.semaphore_wait(barrier, len(peers))
        GB[h] = g_ref[...]
        for d in range(1, NH):
            gains.append(send(g_ref, GB.at[h], g_s.at[d - 1], g_r.at[d - 1], at_h(d)))

    stages = {"a": stage_a, "b": stage_b, "s": send_a, "c": stage_c, "l": stage_l, "d": stage_d, "x": stage_x,
              "y": stage_y, "f": stage_f, "g": stage_g, "h": stage_h, "q": stage_q, "w": stage_w}
    for step in ORDER:
        stages[step[0]](int(step[1]))
    for cp in own:
        cp.wait()
    arrive([cp for cp in sent if id(cp) not in arrived])
    for cp in sent:
        cp.wait_send()


def per_device(queries, keys, values, spikes, gain):
    vmem, dma = pltpu.VMEM, pltpu.SemaphoreType.DMA
    anywhere = pl.BlockSpec(memory_space=pl.ANY)
    inside = pl.BlockSpec(memory_space=pltpu.VMEM)
    state = vmem((NK, NY, HD, HD), f32)
    pair = vmem((NK, NC, NY, HD, HD), f32)
    code = vmem((NK, NY, HD, HD), jnp.int16)
    top = vmem((NK, NY, 1, HD), f32)
    slices = vmem((NK, NZ, ZR, HD), f32)
    rows16, head16 = vmem((NK, NH, ROWS, HD), bf16), vmem((NH, ROWS, HD), bf16)
    over_y, over_z, over_h = (NK, NY - 1, 2), (NK, NZ - 1), (NH - 1,)
    counts = over_h, (NK,), over_y, over_z, (NK, NX - 1), over_z, over_y, (NK,), (NK, NH - 1), over_h, over_h
    attended, cache = pl.pallas_call(
        kernel,
        out_shape=(vmem((BLOCK, NK * HD), bf16), vmem((1, NK, HD, HD), f32)),
        in_specs=[anywhere] * 4 + [inside],
        out_specs=(inside, inside),
        scratch_shapes=[
            rows16, rows16, rows16, vmem((NK, NH, ROWS, HD), jnp.int32), vmem((NK, NH, ROWS, HD), f32),
            pair, vmem((NK * NC, NY, HD, HD), f32), code, top, code, top, state,
            slices, slices, vmem((NK, ZR, HD), f32), vmem((NK, NX, ZR, HD), f32), slices, slices,
            vmem((NY, HD, HD), f32), code, top, code, top, pair, state, rows16, vmem((NH, NK, HD), f32),
            head16, head16, head16, head16, dma((NK, 4)), dma((NK + NH,)),
        ] + [dma(n) for n in counts for _ in range(2)],
        compiler_params=pltpu.CompilerParams(collective_id=0, has_side_effects=True, vmem_limit_bytes=60 << 20),
    )(queries, keys, values, spikes, gain.reshape(NK, HD))
    return attended, cache


def solution(mesh):
    tokens = P(("seq", "head"), None)
    return jax.shard_map(
        per_device, mesh=mesh, in_specs=(tokens, tokens, tokens, tokens, P("head")),
        out_specs=(P("seq", "head"), P("seq", "head", None, None)), check_vma=False,
    )
```

```python
import functools

import jax
import jax.numpy as jnp
from jax import lax
from jax.experimental import pallas as pl
from jax.experimental.pallas import tpu as pltpu
from jax.sharding import PartitionSpec as P

HD = 128
NX, NZ, NY, NC = 4, 8, 4, 2
NH = NY * NC
NK = 4
ROWS = 256
BLOCK = 2048
ZR = HD // NZ
SCALE = HD ** (-0.5)
OWN = 2
ORDER = (
    "a0", "b0", "s0", "a1", "s1", "c0", "a2", "s2", "c1", "a3", "s3", "c2", "c3", "q3",
    "l3", "m3", "d0", "d1", "l2", "d2", "d3", "x0", "x1", "l0", "y0", "x2", "y1", "q2",
    "l1", "x3", "y2", "f0", "y3", "f1", "m2", "g0", "f2", "f3", "h0", "g1", "h1", "w3",
    "w2",
)
f32, bf16 = jnp.float32, jnp.bfloat16


def dot(a, b, dims):
    return lax.dot_general(a, b, (dims, ((), ())), preferred_element_type=f32)


def encode(state):
    top = jnp.max(jnp.abs(state), axis=0, keepdims=True)
    scaled = state * jnp.where(top > 0.0, 1.0 / jnp.where(top > 0.0, top, 1.0), 0.0) * 32767.0
    return jnp.floor(scaled + 0.5).astype(jnp.int32).astype(jnp.int16), top


def decode_state(code, top):
    return code.astype(jnp.int32).astype(f32) * (1.0 / 32767.0) * top


def kernel(q_ref, k_ref, v_ref, sp_ref, g_ref, out_ref, cache_ref,
           qb, kb, vb, sb, lb, S, RC, CC, CM, RT, RM, T1, TZ, Z1, ZT, XB, E2, EB, PB, PC, PM, T3, TM, PF, SP, OB, GB,
           QX, LO, LX, WO,
           in_sem, own_sem, g_s, g_r, c1_s, c1_r, t1_s, t1_r, z1_s, z1_r, x_s, x_r, z2_s, z2_r,
           t3_s, t3_r, c2_s, c2_r, o_s, o_r, q_s, q_r, l_s, l_r):
    s = lax.axis_index("seq")
    h = lax.axis_index("head")
    x, z = s // NZ, s % NZ
    y, c = h // NC, h % NC

    def at_y(d):
        return s, ((y + d) % NY) * NC + c

    def at_h(d):
        return s, (h + d) % NH

    def at_z(d):
        return x * NZ + (z + d) % NZ, h

    def at_x(d):
        return ((x + d) % NX) * NZ + z, h

    partner = (s, y * NC + 1 - c)

    def dev(p):
        return {"seq": p[0], "head": p[1]}

    sent, own, gains, arrived = [], [], [], set()

    def arrive(copies):
        for cp in copies:
            cp.wait_recv()
            arrived.add(id(cp))

    def send(src, dst, ss, rs, to):
        cp = pltpu.make_async_remote_copy(src_ref=src, dst_ref=dst, send_sem=ss, recv_sem=rs,
                                          device_id=dev(to), device_id_type=pl.DeviceIdType.MESH)
        cp.start()
        sent.append(cp)
        return cp

    peers = [at_h(d) for d in range(1, NH)] + [at_z(d) for d in range(1, NZ)] + [at_x(d) for d in range(1, NX)]
    barrier = pltpu.get_barrier_semaphore()
    for p in peers:
        pl.semaphore_signal(barrier, inc=1, device_id=dev(p), device_id_type=pl.DeviceIdType.MESH)

    arrays = ((sp_ref, sb), (q_ref, qb), (k_ref, kb), (v_ref, vb))
    for k in range(NK):
        for a, (src, dst) in enumerate(arrays):
            for g in range(NH):
                pltpu.make_async_copy(src.at[:, pl.ds((g * NK + k) * HD, HD)], dst.at[k, g], in_sem.at[k, a]).start()

    c1, t1, z1, xc, z2, t3, c2, oc, ql = ({} for _ in range(9))

    def stage_a(k):
        for a, (src, dst) in enumerate(arrays):
            pltpu.make_async_copy(dst.at[k], dst.at[k], in_sem.at[k, a]).wait()

        def decode(i, _):
            g = i // 4
            rows = pl.ds(pl.multiple_of((i % 4) * 64, 64), 64)
            t = sb[k, g, rows, :].astype(f32)
            cv = jnp.floor(t * 0.1112)
            r = t - 9.0 * cv
            ck = jnp.floor(r * 0.334)
            cq = r - 3.0 * ck
            qb[k, g, rows, :] = qb[k, g, rows, :] * cq.astype(bf16)
            kb[k, g, rows, :] = kb[k, g, rows, :] * ck.astype(bf16)
            vb[k, g, rows, :] = vb[k, g, rows, :] * cv.astype(bf16)
            return 0

        lax.fori_loop(0, NH * 4, decode, 0, unroll=2)

        def states(yy, _):
            for cc in range(NC):
                S[k, cc, yy] = dot(vb[k, yy * NC + cc], kb[k, yy * NC + cc], ((0,), (0,)))
            return 0

        lax.fori_loop(0, NY, states, 0)

    def send_a(k):
        if k >= OWN:
            c1[k] = send(S.at[k], RC.at[pl.ds(2 * k, 2)], c1_s.at[k], c1_r.at[k], partner)
        else:
            c1[k] = send(S.at[k, 1 - c], RC.at[2 * k + 1 - c], c1_s.at[k], c1_r.at[k], partner)

    def stage_c(k):
        arrive([c1[k]])
        for yy in range(NY):
            CC[k, yy], CM[k, yy] = encode(S[k, c, yy] + RC[2 * k + c, yy])
        t1[k] = []
        for d in range(1, NY):
            to = (y + d) % NY
            t1[k].append(send(CC.at[k, to], RT.at[k, y], t1_s.at[k, d - 1, 0], t1_r.at[k, d - 1, 0], at_y(d)))
            t1[k].append(send(CM.at[k, to], RM.at[k, y], t1_s.at[k, d - 1, 1], t1_r.at[k, d - 1, 1], at_y(d)))
        RT[k, y] = CC[k, y]
        RM[k, y] = CM[k, y]

    def apply_state(q, state):
        hi = state.astype(bf16)
        lo = (state - hi.astype(f32)).astype(bf16)
        return dot(jnp.concatenate([q, q], axis=1), jnp.concatenate([hi, lo], axis=1), ((1,), (1,))) * SCALE

    def stage_l(k):
        causal = lax.broadcasted_iota(jnp.int32, (ROWS, ROWS), 0) >= lax.broadcasted_iota(jnp.int32, (ROWS, ROWS), 1)
        second = c.astype(f32)

        def local(yy, _):
            for cc in range(NC):
                g = yy * NC + cc
                scores = dot(qb[k, g], kb[k, g], ((1,), (1,))) * SCALE
                weights = jnp.where(causal, scores, 0.0).astype(bf16)
                part = dot(weights, vb[k, g], ((1,), (0,)))
                if k >= OWN:
                    part = part + apply_state(qb[k, g], RC[2 * k + cc, yy] * second)
                    LO[k - OWN, g] = part.astype(bf16)
                else:
                    lb[k, g] = part
            return 0

        lax.fori_loop(0, NY, local, 0, unroll=2)

    def stage_m(k):
        e = k - OWN
        for d in range(1, NH):
            ql[k].append(send(LO.at[e, (h + d) % NH], LX.at[e, h], l_s.at[e, d - 1], l_r.at[e, d - 1], at_h(d)))
        LX[e, h] = LO[e, h]

    def stage_q(k):
        e = k - OWN
        ql[k] = [send(qb.at[k, (h + d) % NH], QX.at[e, h], q_s.at[e, d - 1], q_r.at[e, d - 1], at_h(d)) for d in range(1, NH)]
        QX[e, h] = qb[k, h]

    def stage_d(k):
        arrive(t1[k])
        total = None
        for yy in range(NY):
            part = decode_state(RT[k, yy], RM[k, yy])
            T1[k, yy] = part
            total = part if total is None else total + part
        TZ[k] = total.reshape(NZ, ZR, HD)
        z1[k] = [send(TZ.at[k, (z + d) % NZ], Z1.at[k, z], z1_s.at[k, d - 1], z1_r.at[k, d - 1], at_z(d)) for d in range(1, NZ)]
        Z1[k, z] = TZ[k, z]

    def stage_x(k):
        arrive(z1[k])
        total = Z1[k, 0]
        for zz in range(1, NZ):
            total = total + Z1[k, zz]
        ZT[k] = total
        xc[k] = [send(ZT.at[k], XB.at[k, x], x_s.at[k, d - 1], x_r.at[k, d - 1], at_x(d)) for d in range(1, NX)]
        XB[k, x] = total

    def stage_y(k):
        arrive(xc[k])
        run = jnp.zeros((ZR, HD), f32)
        for xx in range(NX - 1):
            run = run + jnp.where(xx < x, XB[k, xx], 0.0)
        for zz in range(NZ):
            E2[k, zz] = run
            run = run + Z1[k, zz]
        z2[k] = [send(E2.at[k, (z + d) % NZ], EB.at[k, z], z2_s.at[k, d - 1], z2_r.at[k, d - 1], at_z(d)) for d in range(1, NZ)]
        EB[k, z] = E2[k, z]

    def stage_f(k):
        arrive(z2[k])
        run = EB[k].reshape(HD, HD)
        for yy in range(NY):
            if k >= OWN:
                PB[k - OWN, yy] = run
            else:
                PC[k, yy], PM[k, yy] = encode(run)
            run = run + T1[k, yy]
        t3[k] = []
        if k < OWN:
            for d in range(1, NY):
                to = (y + d) % NY
                t3[k].append(send(PC.at[k, to], T3.at[k, y], t3_s.at[k, d - 1, 0], t3_r.at[k, d - 1, 0], at_y(d)))
                t3[k].append(send(PM.at[k, to], TM.at[k, y], t3_s.at[k, d - 1, 1], t3_r.at[k, d - 1, 1], at_y(d)))
            T3[k, y] = PC[k, y]
            TM[k, y] = PM[k, y]
        seen = jnp.full((8, HD), (s + 1) * BLOCK, jnp.int32).astype(f32)
        cache_ref[0, k] = (run.T.reshape(HD // 8, 8, HD) * lax.rsqrt(seen)).reshape(HD, HD)

    def stage_g(k):
        arrive(t3[k])
        for yy in range(NY):
            base = decode_state(T3[k, yy], TM[k, yy])
            after = base + jnp.where(c == 0, S[k, 0, yy], RC[2 * k + 1, yy])
            PF[k, c, yy] = jnp.where(c == 0, base, after)
            SP[k, yy] = jnp.where(c == 0, after, base)
        c2[k] = send(SP.at[k], PF.at[k, c], c2_s.at[k], c2_r.at[k], partner)

    def normed(raw, gain):
        mean = jnp.mean(raw * raw, axis=-1, keepdims=True)
        return (raw * lax.rsqrt(mean + 1e-06) * gain).astype(bf16)

    def stage_h(k):
        arrive([c2[k]] + gains if k == 0 else [c2[k]])

        def final(yy, _):
            for cc in range(NC):
                g = yy * NC + cc
                OB[k, g] = normed(lb[k, g] + apply_state(qb[k, g], PF[k, cc, yy]), GB[g, pl.ds(k, 1), :])
            return 0

        lax.fori_loop(0, NY, final, 0, unroll=2)
        here = out_ref.at[pl.ds(h * ROWS, ROWS), pl.ds(k * HD, HD)]
        oc[k] = [send(OB.at[k, (h + d) % NH], here, o_s.at[k, d - 1], o_r.at[k, d - 1], at_h(d)) for d in range(1, NH)]
        mine = pltpu.make_async_copy(OB.at[k, h], here, own_sem.at[k])
        mine.start()
        own.append(mine)

    def stage_w(k):
        arrive(ql[k])
        e = k - OWN

        def final(yy, _):
            for cc in range(NC):
                g = yy * NC + cc
                WO[e, g] = normed(LX[e, g].astype(f32) + apply_state(QX[e, g], PB[e, yy]), g_ref[pl.ds(k, 1), :])
            return 0

        lax.fori_loop(0, NY, final, 0, unroll=2)
        for g in range(NH):
            mine = pltpu.make_async_copy(WO.at[e, g], out_ref.at[pl.ds(g * ROWS, ROWS), pl.ds(k * HD, HD)], own_sem.at[NK + e * NH + g])
            mine.start()
            own.append(mine)

    def stage_b(_):
        pl.semaphore_wait(barrier, len(peers))
        GB[h] = g_ref[...]
        for d in range(1, NH):
            gains.append(send(g_ref, GB.at[h], g_s.at[d - 1], g_r.at[d - 1], at_h(d)))

    stages = {"a": stage_a, "b": stage_b, "s": send_a, "c": stage_c, "l": stage_l, "d": stage_d, "x": stage_x,
              "y": stage_y, "f": stage_f, "g": stage_g, "h": stage_h, "q": stage_q, "w": stage_w, "m": stage_m}
    for step in ORDER:
        stages[step[0]](int(step[1]))
    for cp in own:
        cp.wait()
    arrive([cp for cp in sent if id(cp) not in arrived])
    for cp in sent:
        cp.wait_send()


def per_device(queries, keys, values, spikes, gain):
    vmem, dma = pltpu.VMEM, pltpu.SemaphoreType.DMA
    anywhere = pl.BlockSpec(memory_space=pl.ANY)
    inside = pl.BlockSpec(memory_space=pltpu.VMEM)
    state = vmem((NK, NY, HD, HD), f32)
    pair = vmem((NK, NC, NY, HD, HD), f32)
    code = vmem((NK, NY, HD, HD), jnp.int16)
    top = vmem((NK, NY, 1, HD), f32)
    slices = vmem((NK, NZ, ZR, HD), f32)
    rows16, head16 = vmem((NK, NH, ROWS, HD), bf16), vmem((NK - OWN, NH, ROWS, HD), bf16)
    over_y, over_z, over_h = (NK, NY - 1, 2), (NK, NZ - 1), (NK - OWN, NH - 1)
    counts = (NH - 1,), (NK,), over_y, over_z, (NK, NX - 1), over_z, over_y, (NK,), (NK, NH - 1), over_h, over_h
    attended, cache = pl.pallas_call(
        kernel,
        out_shape=(vmem((BLOCK, NK * HD), bf16), vmem((1, NK, HD, HD), f32)),
        in_specs=[anywhere] * 4 + [inside],
        out_specs=(inside, inside),
        scratch_shapes=[
            rows16, rows16, rows16, vmem((NK, NH, ROWS, HD), jnp.int32), vmem((NK, NH, ROWS, HD), f32),
            pair, vmem((NK * NC, NY, HD, HD), f32), code, top, code, top, state,
            slices, slices, vmem((NK, ZR, HD), f32), vmem((NK, NX, ZR, HD), f32), slices, slices,
            vmem((NK - OWN, NY, HD, HD), f32), code, top, code, top, pair, state, rows16, vmem((NH, NK, HD), f32),
            head16, head16, head16, head16, dma((NK, 4)), dma((NK + (NK - OWN) * NH,)),
        ] + [dma(n) for n in counts for _ in range(2)],
        compiler_params=pltpu.CompilerParams(collective_id=0, has_side_effects=True, vmem_limit_bytes=60 << 20),
    )(queries, keys, values, spikes, gain.reshape(NK, HD))
    return attended, cache


def solution(mesh):
    tokens = P(("seq", "head"), None)
    return jax.shard_map(
        per_device, mesh=mesh, in_specs=(tokens, tokens, tokens, tokens, P("head")),
        out_specs=(P("seq", "head"), P("seq", "head", None, None)), check_vma=False,
    )
```
